256 devices in a mesh: dp: 8 (over z), expert: 32 (over x, y, core).
Axes of the slice: x: 4, y: 4, z: 8, core: 2. Of those that a mesh axis runs over, the one named last changes fastest.
Arguments:
- tokens: bfloat16 [32768, 7168], P(('dp', 'expert')), may hold values from -8 to 8
- routes: int32 [32768, 8], P(('dp', 'expert')), may hold values from 0 to 255, as said below
- slots: int32 [32768, 8], P(('dp', 'expert')), may hold values from 0 to 127, as said below
- gate_weight: bfloat16 [7168, 8192], P(None, 'expert'), may hold values from -0.0625 to 0.0625
- up_weight: bfloat16 [7168, 8192], P(None, 'expert'), may hold values from -0.0625 to 0.0625
Outputs:
- means: float32 [8192], P('expert')
- covariance: float32 [8192, 2048], P('expert', 'dp')
The draws below stay inside these ranges and needn't reach their ends.
Inputs may be any that keep to these rules, and one draw needn't show every extreme that they name: `routes`: each row names 8 different experts; every row names expert 256 - 1. slots[t, k] is the number of earlier tokens of the same device (the rows of one device, 128 in a row) whose routes name routes[t, k]. Every expert below 4 fills all 16 of its slots from every device of at least one dp index.
All inputs are finite; a program needn't handle non-finite values.
Results may differ from the reference program's by a relative error of at most 0.0031.
Values may be sent and summed in bfloat16 or wider, within the bound.
A program may use at most 64 MiB of HBM per device.

```python
import jax
import jax.numpy as jnp
from jax import lax

D = 7168
FF = 2048
ROUTED = 256
TOP = 8
TOK_DEV = 128
EXPERTS = 4
CAP = 16
SOURCES = 32
TOKENS = 32768


def route_table(key):
    block_list = TOKENS // TOK_DEV
    noise_key, force_key = jax.random.split(jax.random.fold_in(key, 11))
    random_jitter = jax.random.randint(noise_key, (block_list, TOK_DEV, ROUTED), 0, 1048576)
    block_number = jnp.arange(block_list, dtype=jnp.int32)
    score_boost = -31457 + block_number * 104857 // max(block_list - 1, 1)
    expert_id = jnp.arange(ROUTED, dtype=jnp.int32)
    pending_rows = expert_id < EXPERTS
    router_scores = random_jitter + jnp.where(pending_rows[None, None, :], score_boost[:, None, None], 0)
    order = jax.random.permutation(force_key, EXPERTS)
    replica_ids = jnp.arange(block_list // SOURCES, dtype=jnp.int32)
    chosen = order[replica_ids % EXPERTS]
    forced = jnp.repeat(chosen, SOURCES)
    leading = jnp.arange(TOK_DEV, dtype=jnp.int32) < CAP
    is_forced = expert_id[None, None, :] == forced[:, None, None]
    router_scores = jnp.where(is_forced, jnp.where(leading[None, :, None], 4194304, -4194304), router_scores)
    always_named = expert_id == ROUTED - 1
    router_scores = jnp.where(always_named[None, None, :], 4194304, router_scores)
    router_scores = router_scores * ROUTED + expert_id[None, None, :]
    chosen_ids = lax.top_k(router_scores, TOP)[1]
    return chosen_ids.astype(jnp.int32)


def draw_routes(key, part):
    return route_table(key).reshape(TOKENS, TOP)


def draw_slots(key, part):
    chosen_ids = route_table(key)
    expert_id = jnp.arange(ROUTED, dtype=jnp.int32)
    named = jnp.any(chosen_ids[..., None] == expert_id, axis=2).astype(jnp.int32)
    earlier = jnp.cumsum(named, axis=1) - named
    positions = jnp.take_along_axis(earlier, chosen_ids, axis=2)
    return positions.astype(jnp.int32).reshape(TOKENS, TOP)


def draw_tokens(key, part):
    noise_key, scale_key, shared_key = jax.random.split(jax.random.fold_in(key, 21), 3)
    random_jitter = jax.random.normal(noise_key, (TOKENS, D))
    row_scale = jnp.exp(jax.random.uniform(scale_key, (TOKENS, 1), minval=-0.6, maxval=0.56))
    common = 0.6 * jax.random.normal(shared_key, (1, D))
    values = common + random_jitter * row_scale
    return jnp.clip(values, -8.0, 8.0).astype(jnp.bfloat16)


def block_levels(rng, extent, cuts, least, top_value):
    factor_of = 1.0
    for dim, shards_of in cuts:
        heights = jax.random.uniform(jax.random.fold_in(jax.random.fold_in(rng, 6), dim), (shards_of,), jnp.float32, least / len(cuts), top_value / len(cuts))
        factor_of = factor_of * jnp.repeat(jnp.exp(heights), extent[dim] // shards_of).reshape((-1,) + (1,) * (len(extent) - 1 - dim))
    return factor_of


def normal_values(rng, dims, deviation, reach, cuts=(), kind=jnp.bfloat16):
    array = jax.random.normal(rng, dims, jnp.float32) * deviation
    if len(cuts) > 0:
        array = block_levels(rng, dims, cuts, -0.22, 0.18) * array
    return jnp.clip(array, min=-reach, max=reach).astype(kind)


def setup_inputs(seed: int = 0) -> dict:
    splits = jax.random.split(jax.random.key(seed), 6)
    return {
        "tokens": draw_tokens(jax.random.fold_in(splits[5], 71), 0),
        "routes": draw_routes(jax.random.fold_in(splits[5], 71), 0),
        "slots": draw_slots(jax.random.fold_in(splits[5], 71), 0),
        "gate_weight": normal_values(splits[3], (D, EXPERTS * FF), D ** -0.5, 0.0625, ((1, 32),)),
        "up_weight": normal_values(splits[4], (D, EXPERTS * FF), D ** -0.5, 0.0625, ((1, 32),)),
    }


def reference(tokens, routes, slots, gate_weight, up_weight):
    block_list = TOKENS // TOK_DEV
    token_blocks = tokens.reshape(block_list, TOK_DEV, D)
    usable = (routes < EXPERTS) & (slots < CAP)
    target = jnp.where(usable, routes * CAP + slots, -1).reshape(block_list, TOK_DEV, TOP)
    places = jnp.arange(EXPERTS * CAP, dtype=jnp.int32)

    def pack_block(element):
        block_rows, block_marks = element
        placing = jnp.any(places[:, None, None] == block_marks[None], axis=2)
        return jnp.dot(placing.astype(jnp.bfloat16), block_rows, preferred_element_type=jnp.float32).astype(jnp.bfloat16)

    packed = lax.map(pack_block, (token_blocks, target))
    packed = packed.reshape(block_list, EXPERTS, CAP, D).transpose(1, 0, 2, 3).reshape(EXPERTS, block_list * CAP, D)
    expert_ids = jnp.arange(EXPERTS, dtype=jnp.int32)
    counts = jnp.sum((routes[:, :, None] == expert_ids[None, None, :]) & (slots < CAP)[:, :, None], axis=(0, 1)).astype(jnp.float32)
    gate_stack = gate_weight.reshape(D, EXPERTS, FF).transpose(1, 0, 2)
    up_stack = up_weight.reshape(D, EXPERTS, FF).transpose(1, 0, 2)

    def moments(element):
        expert_rows, gate_cols, up_columns = element
        gate_sums = jnp.dot(expert_rows, gate_cols, preferred_element_type=jnp.float32)
        up_sums = jnp.dot(expert_rows, up_columns, preferred_element_type=jnp.float32)
        hidden = (jax.nn.silu(gate_sums) * up_sums).astype(jnp.bfloat16)
        column_sums = jnp.sum(hidden.astype(jnp.float32), axis=0)
        gram_block = jnp.dot(hidden.T, hidden, preferred_element_type=jnp.float32)
        return column_sums, gram_block

    column_sums, gram_stack = lax.map(moments, (packed, gate_stack, up_stack))
    mean_rows = column_sums / counts[:, None]
    covariance = gram_stack / counts[:, None, None] - mean_rows[:, :, None] * mean_rows[:, None, :]
    return mean_rows.reshape(EXPERTS * FF), covariance.reshape(EXPERTS * FF, FF)
```

```python
import functools

import jax
import jax.numpy as jnp
from jax import lax
from jax.experimental import pallas as pl
from jax.experimental.pallas import tpu as pltpu
from jax.sharding import PartitionSpec as P

MESH = pl.DeviceIdType.MESH
F32 = jnp.float32
BF16 = jnp.bfloat16

CAP = 16
XS = 4
YS = 4
ZS = 8
FLAG = 128
CH = 2 * YS * CAP
COUNT_ROWS = 16


def kernel(
    tok_ref, routes_ref, slots_ref, wg_hbm, wu_hbm, cov_ref, mean_ref,
    packed, rows, wg, wu, hid, hidz, gram, colsum,
    w_sem, l_sem, x_s, x_r, ya_s, ya_r, yb_s, yb_r, sb_s, sb_r,
    z_s, z_r, h_s, h_r, hs_s,
):
    depth = wg.shape[0]
    units = wg.shape[1]
    wide = depth + FLAG
    half = depth // 2
    chunks = XS

    z = lax.axis_index("dp")
    member = lax.axis_index("expert")
    x = member // (2 * YS)
    y = (member // 2) % YS
    c = member % 2

    def dev(dx=0, dy=0, dz=0, dc=0):
        xx = (x + dx) % XS
        yy = (y + dy) % YS
        cc = (c + dc) % 2
        return {"dp": (z + dz) % ZS, "expert": (xx * YS + yy) * 2 + cc}

    peers = [dict(dx=1), dict(dx=2), dict(dx=3), dict(dy=1), dict(dy=3), dict(dc=1), dict(dz=1), dict(dz=7)]
    barrier = pltpu.get_barrier_semaphore()
    for p in peers:
        pl.semaphore_signal(barrier, inc=1, device_id=dev(**p), device_id_type=MESH)
    wg_copy = pltpu.make_async_copy(wg_hbm, wg, w_sem.at[0])
    wu_copy = pltpu.make_async_copy(wu_hbm, wu, w_sem.at[1])
    wg_copy.start()
    wu_copy.start()

    routes = routes_ref[...]
    slots = slots_ref[...]
    usable = (routes < XS) & (slots < CAP)
    target = jnp.where(usable, routes * CAP + slots, -1)
    tok_rows = routes.shape[0]
    places = lax.broadcasted_iota(jnp.int32, (tok_rows, XS * CAP), 1)
    hit = jnp.zeros((tok_rows, XS * CAP), F32)
    for k in range(routes.shape[1]):
        hit = jnp.maximum(hit, jnp.where(target[:, k : k + 1] == places, 1.0, 0.0))
    placing = hit.astype(BF16)

    def tdot(a, b):
        return lax.dot_general(a, b, (((0,), (0,)), ((), ())), preferred_element_type=F32)

    step = depth // 7
    for j in range(7):
        part = tdot(placing, tok_ref[:, j * step : (j + 1) * step]).astype(BF16)
        for g in range(XS):
            packed[g, :, j * step : (j + 1) * step] = part[g * CAP : (g + 1) * CAP]
    flags = tdot(placing, jnp.ones((tok_rows, FLAG), BF16)).astype(BF16)
    for g in range(XS):
        packed[g, :, depth:wide] = flags[g * CAP : (g + 1) * CAP]

    pl.semaphore_wait(barrier, len(peers))

    sends = []

    def send(src, dst, ss, rs, to):
        copy = pltpu.make_async_remote_copy(
            src_ref=src, dst_ref=dst, send_sem=ss, recv_sem=rs, device_id=to, device_id_type=MESH
        )
        copy.start()
        return copy

    def arrived(dst, rs):
        pltpu.make_async_remote_copy(
            src_ref=dst, dst_ref=dst, send_sem=rs, recv_sem=rs, device_id=dev(dc=1), device_id_type=MESH
        ).wait_recv()

    def piece(k, yy, cc):
        start = pl.multiple_of((yy * 2 + cc) * CAP, CAP)
        return rows.at[k, pl.ds(start, CAP), :]

    def half_piece(k, yy, cc, h):
        start = pl.multiple_of((yy * 2 + cc) * CAP, CAP)
        lanes = pl.ds(0, half) if h == 0 else pl.ds(half, wide - half)
        return rows.at[k, pl.ds(start, CAP), lanes]

    y_up, y_dn, y_op = (y + 1) % YS, (y + YS - 1) % YS, (y + 2) % YS

    def stage_a(k):
        if k == 0:
            own = packed.at[x]
        else:
            own = piece(k, y, c)
            arrived(own, x_r.at[k - 1])
        sends.append(send(own, piece(k, y, c), ya_s.at[k, 0], ya_r.at[k, 0], dev(dy=1)))
        sends.append(send(own, piece(k, y, c), ya_s.at[k, 1], ya_r.at[k, 1], dev(dy=3)))
        sends.append(send(own, piece(k, y, c), sb_s.at[k, 0], sb_r.at[k, 0], dev(dc=1)))

    def stage_b(k):
        arrived(piece(k, y_dn, c), ya_r.at[k, 0])
        sends.append(send(half_piece(k, y_dn, c, 0), half_piece(k, y_dn, c, 0), yb_s.at[k, 0], yb_r.at[k, 0], dev(dy=1)))
        sends.append(send(piece(k, y_dn, c), piece(k, y_dn, c), sb_s.at[k, 1], sb_r.at[k, 1], dev(dc=1)))
        arrived(piece(k, y_up, c), ya_r.at[k, 1])
        sends.append(send(half_piece(k, y_up, c, 1), half_piece(k, y_up, c, 1), yb_s.at[k, 1], yb_r.at[k, 1], dev(dy=3)))
        sends.append(send(piece(k, y_up, c), piece(k, y_up, c), sb_s.at[k, 2], sb_r.at[k, 2], dev(dc=1)))

    def stage_c(k):
        arrived(half_piece(k, y_op, c, 0), yb_r.at[k, 0])
        arrived(half_piece(k, y_op, c, 1), yb_r.at[k, 1])
        sends.append(send(piece(k, y_op, c), piece(k, y_op, c), sb_s.at[k, 3], sb_r.at[k, 3], dev(dc=1)))

    def hrows(k):
        n = CH + (COUNT_ROWS if k == chunks - 1 else 0)
        return pl.ds(k * CH, n)

    def hslot(k, s):
        return hid.at[s, hrows(k), :]

    def hhalf(k, h):
        n = CH // 2 + (COUNT_ROWS if (k == chunks - 1 and h == 1) else 0)
        return hid.at[4, pl.ds(k * CH + h * (CH // 2), n), :]

    def hhalf_of(k, s, h):
        n = CH // 2 + (COUNT_ROWS if (k == chunks - 1 and h == 1) else 0)
        return hid.at[s, pl.ds(k * CH + h * (CH // 2), n), :]

    def stage_d(k):
        for i, yy in enumerate((y, y_dn, y_up, y_op)):
            arrived(piece(k, yy, (c + 1) % 2), sb_r.at[k, i])
        if k == 0:
            wg_copy.wait()
            wu_copy.wait()
        lhs = rows[k, :, 0:depth]
        gate = jnp.dot(lhs, wg[...], preferred_element_type=F32)
        up = jnp.dot(lhs, wu[...], preferred_element_type=F32)
        hid[0, k * CH : (k + 1) * CH, :] = (gate / (1.0 + jnp.exp(-gate)) * up).astype(BF16)
        if k == chunks - 1:
            for r in range(chunks):
                used = jnp.sum(rows[r, :, depth:wide].astype(F32), axis=0, keepdims=True)
                used = jnp.concatenate([used, used], axis=1)
                hid[0, chunks * CH + 4 * r : chunks * CH + 4 * (r + 1), :] = jnp.broadcast_to(used, (4, units)).astype(BF16)
        sends.append(send(hslot(k, 0), hslot(k, 1), z_s.at[k, 0, 0], z_r.at[k, 0, 0], dev(dz=1)))
        sends.append(send(hslot(k, 0), hslot(k, 7), z_s.at[k, 0, 1], z_r.at[k, 0, 1], dev(dz=7)))

    def stage_z(k, t):
        arrived(hslot(k, t), z_r.at[k, t - 1, 0])
        if t < 3:
            sends.append(send(hslot(k, t), hslot(k, t + 1), z_s.at[k, t, 0], z_r.at[k, t, 0], dev(dz=1)))
        else:
            sends.append(send(hhalf_of(k, 3, 0), hhalf(k, 0), z_s.at[k, 3, 0], z_r.at[k, 3, 0], dev(dz=1)))
        arrived(hslot(k, 8 - t), z_r.at[k, t - 1, 1])
        if t < 3:
            sends.append(send(hslot(k, 8 - t), hslot(k, 7 - t), z_s.at[k, t, 1], z_r.at[k, t, 1], dev(dz=7)))
        else:
            sends.append(send(hhalf_of(k, 5, 1), hhalf(k, 1), z_s.at[k, 3, 1], z_r.at[k, 3, 1], dev(dz=7)))

    def stage_z5(k):
        arrived(hhalf(k, 0), z_r.at[k, 3, 0])
        arrived(hhalf(k, 1), z_r.at[k, 3, 1])

    d = (y + YS - z // 2) % YS
    on_line = c == z % 2

    def bpart(ref, k, h):
        return ref.at[pl.ds(4 * h, 4), pl.ds(k * CH, CH), :]

    def bcopy(src, k, h, to_y):
        if to_y:
            ss, to = h_s.at[k, h], dev(dy=1 if h == 0 else 3)
        else:
            ss, to = hs_s.at[k, h], dev(dc=1)
        return pltpu.make_async_remote_copy(
            src_ref=bpart(src, k, h), dst_ref=bpart(hidz, k, h), send_sem=ss, recv_sem=h_r.at[k, h],
            device_id=to, device_id_type=MESH,
        )

    def own_copy(k):
        return pltpu.make_async_copy(
            hid.at[:, pl.ds(k * CH, CH), :], hidz.at[:, pl.ds(k * CH, CH), :], l_sem.at[k]
        )

    def bforward(k, h, to_y):
        arrived(bpart(hidz, k, h), h_r.at[k, h])
        if to_y:
            bcopy(hidz, k, h, True).start()
        bcopy(hidz, k, h, False).start()

    def stage_y1(k):
        @pl.when(on_line & (d == 0))
        def _():
            for h in range(2):
                bcopy(hid, k, h, True).start()
            for h in range(2):
                bcopy(hid, k, h, False).start()
            own_copy(k).start()

    def stage_y2(k):
        @pl.when(on_line & (d == 1))
        def _():
            bforward(k, 0, True)

        @pl.when(on_line & (d == 3))
        def _():
            bforward(k, 1, True)

    def stage_y3(k):
        @pl.when(on_line & (d == 2))
        def _():
            bforward(k, 0, True)
            bforward(k, 1, True)

    def stage_y4(k):
        @pl.when(on_line & (d == 1))
        def _():
            bforward(k, 1, False)

        @pl.when(on_line & (d == 3))
        def _():
            bforward(k, 0, False)

        @pl.when(on_line & (d == 0))
        def _():
            own_copy(k).wait()

        @pl.when(jnp.logical_not(on_line))
        def _():
            arrived(bpart(hidz, k, 0), h_r.at[k, 0])
            arrived(bpart(hidz, k, 1), h_r.at[k, 1])

        n = ZS * CH
        a = hid[:, k * CH : (k + 1) * CH, :].reshape(n, units)
        b = hidz[:, k * CH : (k + 1) * CH, :].reshape(n, units)
        ones_l = jnp.ones((n, 128), BF16)
        ones_s = jnp.ones((8, n), BF16)
        g_part = tdot(a, jnp.concatenate([b, ones_l], axis=1))
        s_part = jnp.dot(ones_s, jnp.concatenate([a, b], axis=1), preferred_element_type=F32)
        if k == 0:
            gram[...] = g_part
            colsum[...] = s_part
        else:
            gram[...] += g_part
            colsum[...] += s_part

    stage_a(0)
    for k, dx in ((1, 1), (2, 3), (3, 2)):
        sends.append(send(packed.at[(x + dx) % XS], piece(k, y, c), x_s.at[k - 1], x_r.at[k - 1], dev(dx=dx)))
    own_rows = pl.multiple_of((y * 2 + c) * CAP, CAP)
    rows[0, pl.ds(own_rows, CAP), :] = packed[x]

    stage_a(1)
    stage_b(0)
    stage_a(2)
    stage_c(0)
    stage_d(0)

    stage_b(1)
    stage_a(3)
    stage_z(0, 1)
    stage_c(1)
    stage_z(0, 2)
    stage_d(1)
    stage_z(0, 3)

    stage_b(2)
    stage_z5(0)
    stage_y1(0)
    stage_z(1, 1)
    stage_c(2)
    stage_y2(0)
    stage_z(1, 2)
    stage_d(2)
    stage_y3(0)
    stage_z(1, 3)

    stage_b(3)
    stage_z5(1)
    stage_y1(1)
    stage_z(2, 1)
    stage_c(3)
    stage_y2(1)
    stage_z(2, 2)
    stage_d(3)
    stage_y4(0)
    stage_y3(1)
    stage_z(2, 3)

    stage_z5(2)
    stage_y1(2)
    stage_z(3, 1)
    stage_y2(2)
    stage_y4(1)
    stage_z(3, 2)
    stage_y3(2)
    stage_z(3, 3)
    stage_y4(2)
    stage_z5(3)
    stage_y1(3)
    stage_y2(3)
    stage_y3(3)
    stage_y4(3)

    used = hid[:, chunks * CH : chunks * CH + COUNT_ROWS, 0:128].astype(F32)
    count = jnp.sum(used) * (1.0 / (4 * 128))
    mean_ref[...] = colsum[:, 0:units] / count
    row_mean = gram[:, units : units + 1] / count
    col_mean = colsum[0:1, units:] / count
    cov_ref[...] = gram[:, 0:units] / count - row_mean * col_mean

    for copy in sends:
        copy.wait_send()
    for k in range(chunks):
        @pl.when(on_line & (d != 3))
        def _():
            bcopy(hidz, k, 0, True).wait_send()

        @pl.when(on_line & (d != 1))
        def _():
            bcopy(hidz, k, 1, True).wait_send()

        @pl.when(on_line)
        def _():
            bcopy(hidz, k, 0, False).wait_send()
            bcopy(hidz, k, 1, False).wait_send()


def local(tokens, routes, slots, gate_weight, up_weight):
    tok_rows, depth = tokens.shape
    units = gate_weight.shape[1]
    hrows = XS * CH + COUNT_ROWS
    vmem = pl.BlockSpec(memory_space=pltpu.VMEM)
    hbm = pl.BlockSpec(memory_space=pl.ANY)
    dma = pltpu.SemaphoreType.DMA
    cov, means = pl.pallas_call(
        kernel,
        out_shape=(
            jax.ShapeDtypeStruct((units, units), F32),
            jax.ShapeDtypeStruct((8, units), F32),
        ),
        in_specs=[vmem, vmem, vmem, hbm, hbm],
        out_specs=(vmem, vmem),
        scratch_shapes=[
            pltpu.VMEM((XS, CAP, depth + FLAG), BF16),
            pltpu.VMEM((XS, CH, depth + FLAG), BF16),
            pltpu.VMEM((depth, units), BF16),
            pltpu.VMEM((depth, units), BF16),
            pltpu.VMEM((ZS, hrows, units), BF16),
            pltpu.VMEM((ZS, hrows, units), BF16),
            pltpu.VMEM((units, units + 128), F32),
            pltpu.VMEM((8, 2 * units), F32),
            dma((2,)), dma((XS,)),
            dma((3,)), dma((3,)),
            dma((XS, 2)), dma((XS, 2)),
            dma((XS, 2)), dma((XS, 2)),
            dma((XS, 4)), dma((XS, 4)),
            dma((XS, 4, 2)), dma((XS, 4, 2)),
            dma((XS, 2)), dma((XS, 2)), dma((XS, 2)),
        ],
        compiler_params=pltpu.CompilerParams(
            collective_id=0, has_side_effects=True, vmem_limit_bytes=48 << 20
        ),
        name="moments",
    )(tokens, routes, slots, gate_weight, up_weight)
    return means[0], cov


def solution(mesh):
    in_specs = (
        P(("dp", "expert"), None),
        P(("dp", "expert"), None),
        P(("dp", "expert"), None),
        P(None, "expert"),
        P(None, "expert"),
    )
    out_specs = (P("expert"), P("expert", "dp"))
    return jax.shard_map(local, mesh=mesh, in_specs=in_specs, out_specs=out_specs, check_vma=False)
```

```python
import functools

import jax
import jax.numpy as jnp
from jax import lax
from jax.experimental import pallas as pl
from jax.experimental.pallas import tpu as pltpu
from jax.sharding import PartitionSpec as P

MESH = pl.DeviceIdType.MESH
F32 = jnp.float32
BF16 = jnp.bfloat16

CAP = 16
XS = 4
YS = 4
ZS = 8
FLAG = 128
CHUNKS = ((0, 0, 16, 0), (1, 0, 16, 128), (3, 0, 16, 256), (2, 0, 8, 384), (2, 8, 8, 448))
ROWS = 2 * XS * YS * CAP
COUNT_ROWS = 16


RELAY = (0, 1)
DIRECT = tuple(k for k in range(len(CHUNKS)) if k not in RELAY)
STRAIGHT = (4,)


def kernel(
    tok_ref, routes_ref, slots_ref, wg_hbm, wu_hbm, cov_ref, mean_ref,
    packed, rows, wg, wu, hid, hidz, hidy, gram, colsum,
    w_sem, l_sem, x_s, x_r, ya_s, ya_r, yb_s, yb_r, sb_s, sb_r,
    z_s, z_r, zd_s, zd_r, h_s, h_r, hs_s, ye_s, ye_r, e_s, e_r, t_s, t_r,
):
    depth = wg.shape[0]
    units = wg.shape[1]
    wide = depth + FLAG
    half = depth // 2
    last = len(CHUNKS) - 1

    z = lax.axis_index("dp")
    member = lax.axis_index("expert")
    x = member // (2 * YS)
    y = (member // 2) % YS
    c = member % 2

    def dev(dx=0, dy=0, dz=0, dc=0):
        xx = (x + dx) % XS
        yy = (y + dy) % YS
        cc = (c + dc) % 2
        return {"dp": (z + dz) % ZS, "expert": (xx * YS + yy) * 2 + cc}

    peers = [dict(dx=1), dict(dx=2), dict(dx=3), dict(dy=1), dict(dy=2), dict(dy=3), dict(dc=1)]
    peers += [dict(dz=s) for s in range(1, ZS)]
    barrier = pltpu.get_barrier_semaphore()
    for p in peers:
        pl.semaphore_signal(barrier, inc=1, device_id=dev(**p), device_id_type=MESH)
    on_line = c == z % 2
    wg_copy = pltpu.make_async_copy(wg_hbm, wg, w_sem.at[0])
    wu_copy = pltpu.make_async_copy(wu_hbm, wu, w_sem.at[1])
    wg_copy.start()
    wu_copy.start()

    routes = routes_ref[...]
    slots = slots_ref[...]
    usable = (routes < XS) & (slots < CAP)
    target = jnp.where(usable, routes * CAP + slots, -1)
    tok_rows = routes.shape[1]
    places = lax.broadcasted_iota(jnp.int32, (XS * CAP, tok_rows), 0)
    hit = jnp.zeros((XS * CAP, tok_rows), F32)
    for k in range(routes.shape[0]):
        hit = jnp.maximum(hit, jnp.where(target[k : k + 1, :] == places, 1.0, 0.0))
    placing = hit.astype(BF16)

    def tdot(a, b):
        return lax.dot_general(a, b, (((0,), (0,)), ((), ())), preferred_element_type=F32)

    step = depth // 7
    for j in range(7):
        part = jnp.dot(placing, tok_ref[:, j * step : (j + 1) * step], preferred_element_type=F32).astype(BF16)
        for g in range(XS):
            packed[g, :, j * step : (j + 1) * step] = part[g * CAP : (g + 1) * CAP]
    flags = jnp.dot(placing, jnp.ones((tok_rows, FLAG), BF16), preferred_element_type=F32).astype(BF16)
    for g in range(XS):
        packed[g, :, depth:wide] = flags[g * CAP : (g + 1) * CAP]

    gram[...] = jnp.zeros_like(gram)
    colsum[...] = jnp.zeros_like(colsum)
    pl.semaphore_wait(barrier, len(peers))

    sends = []

    def send(src, dst, ss, rs, to):
        copy = pltpu.make_async_remote_copy(
            src_ref=src, dst_ref=dst, send_sem=ss, recv_sem=rs, device_id=to, device_id_type=MESH
        )
        copy.start()
        return copy

    def arrived(dst, rs):
        pltpu.make_async_remote_copy(
            src_ref=dst, dst_ref=dst, send_sem=rs, recv_sem=rs, device_id=dev(dc=1), device_id_type=MESH
        ).wait_recv()

    def size(k):
        return 2 * YS * CHUNKS[k][2]

    def piece_rows(k, yy, cc):
        n = CHUNKS[k][2]
        return pl.ds(pl.multiple_of(CHUNKS[k][3] + (yy * 2 + cc) * n, n), n)

    def lanes(h):
        return pl.ds(0, half) if h == 0 else pl.ds(half, wide - half)

    def piece(k, yy, cc):
        return rows.at[piece_rows(k, yy, cc), :]

    def half_piece(k, yy, cc, h):
        return rows.at[piece_rows(k, yy, cc), lanes(h)]

    y_up, y_dn, y_op = (y + 1) % YS, (y + YS - 1) % YS, (y + 2) % YS

    def stage_a(k):
        dx, lo, n, _ = CHUNKS[k]
        if dx == 0:
            own = packed.at[x, pl.ds(lo, n), :]
        else:
            own = piece(k, y, c)
            arrived(own, x_r.at[k])
        for i in range(2):
            for way in range(2):
                h = way if i == 0 else 1 - way
                src = packed.at[x, pl.ds(lo, n), lanes(h)] if dx == 0 else half_piece(k, y, c, h)
                to = dev(dy=1 if way == 0 else 3)
                sends.append(send(src, half_piece(k, y, c, h), ya_s.at[k, way, i], ya_r.at[k, way, i], to))
        sends.append(send(own, piece(k, y, c), sb_s.at[k, 0], sb_r.at[k, 0], dev(dc=1)))

    def stage_b(k):
        for way, yy in enumerate((y_dn, y_up)):
            part = half_piece(k, yy, c, way)
            arrived(part, ya_r.at[k, way, 0])
            sends.append(send(part, part, yb_s.at[k, way], yb_r.at[k, way], dev(dy=1 if way == 0 else 3)))

    def stage_s(k):
        for way, yy in enumerate((y_dn, y_up)):
            arrived(half_piece(k, yy, c, 1 - way), ya_r.at[k, way, 1])
            sends.append(send(piece(k, yy, c), piece(k, yy, c), sb_s.at[k, 1 + way], sb_r.at[k, 1 + way], dev(dc=1)))

    def stage_c(k):
        arrived(half_piece(k, y_op, c, 0), yb_r.at[k, 0])
        arrived(half_piece(k, y_op, c, 1), yb_r.at[k, 1])
        sends.append(send(piece(k, y_op, c), piece(k, y_op, c), sb_s.at[k, 3], sb_r.at[k, 3], dev(dc=1)))

    def hrows(k):
        return pl.ds(CHUNKS[k][3], size(k) + (COUNT_ROWS if k == last else 0))

    def hslot(k, s):
        return hid.at[s, hrows(k), :]

    def hhalf(k, s, h):
        n = size(k) // 2
        return hid.at[s, pl.ds(CHUNKS[k][3] + h * n, n + (COUNT_ROWS if k == last and h == 1 else 0)), :]

    def stage_d(k):
        for i, yy in enumerate((y, y_dn, y_up, y_op)):
            arrived(piece(k, yy, (c + 1) % 2), sb_r.at[k, i])
        if k == 0:
            wg_copy.wait()
            wu_copy.wait()
        at, n = CHUNKS[k][3], size(k)
        lhs = rows[at : at + n, 0:depth]
        gate = jnp.dot(lhs, wg[...], preferred_element_type=F32)
        up = jnp.dot(lhs, wu[...], preferred_element_type=F32)
        hid[0, at : at + n, :] = (gate / (1.0 + jnp.exp(-gate)) * up).astype(BF16)
        if k == last:
            for r in range(4):
                part = ROWS // 4
                used = jnp.sum(rows[r * part : (r + 1) * part, depth:wide].astype(F32), axis=0, keepdims=True)
                used = jnp.concatenate([used, used], axis=1)
                hid[0, ROWS + 4 * r : ROWS + 4 * (r + 1), :] = jnp.broadcast_to(used, (4, units)).astype(BF16)
        if k in STRAIGHT:
            for s in (4, 3, 5, 2, 6, 1, 7):
                sends.append(send(hslot(k, 0), hslot(k, s), zd_s.at[k, s - 1], zd_r.at[k, s - 1], dev(dz=s)))
        else:
            sends.append(send(hslot(k, 0), hslot(k, 1), z_s.at[k, 0, 0], z_r.at[k, 0, 0], dev(dz=1)))
            sends.append(send(hslot(k, 0), hslot(k, 7), z_s.at[k, 0, 1], z_r.at[k, 0, 1], dev(dz=7)))

    def stage_q(k):
        for s in range(1, ZS):
            arrived(hslot(k, s), zd_r.at[k, s - 1])

    def stage_z(k, t):
        arrived(hslot(k, t), z_r.at[k, t - 1, 0])
        if t < 3:
            sends.append(send(hslot(k, t), hslot(k, t + 1), z_s.at[k, t, 0], z_r.at[k, t, 0], dev(dz=1)))
        else:
            sends.append(send(hhalf(k, 3, 0), hhalf(k, 4, 0), z_s.at[k, 3, 0], z_r.at[k, 3, 0], dev(dz=1)))
        arrived(hslot(k, 8 - t), z_r.at[k, t - 1, 1])
        if t < 3:
            sends.append(send(hslot(k, 8 - t), hslot(k, 7 - t), z_s.at[k, t, 1], z_r.at[k, t, 1], dev(dz=7)))
        else:
            sends.append(send(hhalf(k, 5, 1), hhalf(k, 4, 1), z_s.at[k, 3, 1], z_r.at[k, 3, 1], dev(dz=7)))

    def stage_z5(k):
        arrived(hhalf(k, 4, 0), z_r.at[k, 3, 0])
        arrived(hhalf(k, 4, 1), z_r.at[k, 3, 1])

    def accumulate(k):
        at, n = CHUNKS[k][3], ZS * size(k)
        a = hid[:, at : at + size(k), :].reshape(n, units)
        b = hidz[:, at : at + size(k), :].reshape(n, units)
        ones_l = jnp.ones((n, 128), BF16)
        ones_s = jnp.ones((8, n), BF16)
        gram[...] += tdot(a, jnp.concatenate([b, ones_l], axis=1))
        colsum[...] += jnp.dot(ones_s, jnp.concatenate([a, b], axis=1), preferred_element_type=F32)

    d = (y + YS - z // 2) % YS

    def bpart(ref, k, h):
        return ref.at[pl.ds(4 * h, 4), pl.ds(CHUNKS[k][3], size(k)), :]

    def bcopy(src, k, h, to_y):
        if to_y:
            ss, to = h_s.at[k, h], dev(dy=1 if h == 0 else 3)
        else:
            ss, to = hs_s.at[k, h], dev(dc=1)
        return pltpu.make_async_remote_copy(
            src_ref=bpart(src, k, h), dst_ref=bpart(hidz, k, h), send_sem=ss, recv_sem=h_r.at[k, h],
            device_id=to, device_id_type=MESH,
        )

    def own_copy(k):
        return pltpu.make_async_copy(
            hid.at[:, pl.ds(CHUNKS[k][3], size(k)), :], hidz.at[:, pl.ds(CHUNKS[k][3], size(k)), :], l_sem.at[k]
        )

    def bforward(k, h, to_y):
        arrived(bpart(hidz, k, h), h_r.at[k, h])
        if to_y:
            bcopy(hidz, k, h, True).start()
        bcopy(hidz, k, h, False).start()

    def stage_y1(k):
        @pl.when(on_line & (d == 0))
        def _():
            for h in range(2):
                bcopy(hid, k, h, True).start()
            for h in range(2):
                bcopy(hid, k, h, False).start()
            own_copy(k).start()

    def stage_y2(k):
        @pl.when(on_line & (d == 1))
        def _():
            bforward(k, 0, True)

        @pl.when(on_line & (d == 3))
        def _():
            bforward(k, 1, True)

    def stage_y3(k):
        @pl.when(on_line & (d == 2))
        def _():
            bforward(k, 0, True)
            bforward(k, 1, True)

    def stage_y4(k):
        @pl.when(on_line & (d == 1))
        def _():
            bforward(k, 1, False)

        @pl.when(on_line & (d == 3))
        def _():
            bforward(k, 0, False)

        @pl.when(on_line & (d == 0))
        def _():
            own_copy(k).wait()

        @pl.when(jnp.logical_not(on_line))
        def _():
            arrived(bpart(hidz, k, 0), h_r.at[k, 0])
            arrived(bpart(hidz, k, 1), h_r.at[k, 1])

        accumulate(k)

    def krows(ref, k, s):
        return ref.at[s, pl.ds(CHUNKS[k][3], size(k)), :]

    def block_of(j):
        return 2 * ((y + j) % YS) + c

    def held(k, j):
        return krows(hid, k, 0) if j == 0 else krows(hidy, k, j - 1)

    def side_copy(k, i):
        return pltpu.make_async_remote_copy(
            src_ref=krows(hid, k, 0), dst_ref=krows(hidy, k, YS - i - 1), send_sem=ye_s.at[k, i - 1],
            recv_sem=ye_r.at[k, YS - i - 1], device_id=dev(dy=i), device_id_type=MESH,
        )

    def block_copy(k, j):
        block = block_of(j)
        slot = (block + ZS - z) % ZS
        return pltpu.make_async_remote_copy(
            src_ref=held(k, j), dst_ref=krows(hidz, k, slot), send_sem=e_s.at[k, j],
            recv_sem=e_r.at[k, slot], device_id={"dp": block, "expert": member}, device_id_type=MESH,
        )

    def kept_copy(k, j):
        return pltpu.make_async_copy(held(k, j), krows(hidz, k, 0), l_sem.at[k])

    def line_copy(k):
        part = hidz.at[:, pl.ds(CHUNKS[k][3], size(k)), :]
        return pltpu.make_async_remote_copy(
            src_ref=part, dst_ref=part, send_sem=t_s.at[k], recv_sem=t_r.at[k],
            device_id=dev(dc=1), device_id_type=MESH,
        )

    def pass_on(k, j):
        if j > 0:
            arrived(held(k, j), ye_r.at[k, j - 1])

        @pl.when(z == block_of(j))
        def _():
            kept_copy(k, j).start()

        @pl.when(z != block_of(j))
        def _():
            block_copy(k, j).start()

    def stage_e(k):
        for i in (1, 3, 2):
            side_copy(k, i).start()
        pass_on(k, 0)

    def stage_f(k):
        for j in (1, 3, 2):
            pass_on(k, j)

    def stage_w(k):
        @pl.when(on_line)
        def _():
            for s in range(1, ZS):
                arrived(krows(hidz, k, s), e_r.at[k, s])
            kept_copy(k, 0).wait()
            line_copy(k).start()

    def stage_g(k):
        @pl.when(jnp.logical_not(on_line))
        def _():
            line_copy(k).wait_recv()

        accumulate(k)

    stage_a(0)
    for k, (dx, lo, n, _) in enumerate(CHUNKS):
        if dx > 0:
            src = packed.at[(x + dx) % XS, pl.ds(lo, n), :]
            sends.append(send(src, piece(k, y, c), x_s.at[k], x_r.at[k], dev(dx=dx)))
        else:
            rows[piece_rows(k, y, c), :] = packed[x, lo : lo + n]

    stage_b(0)
    stage_s(0)
    stage_a(1)
    stage_c(0)
    stage_b(1)
    stage_d(0)
    stage_a(2)
    stage_s(1)
    stage_a(3)
    stage_c(1)
    stage_z(0, 1)
    stage_d(1)
    stage_b(2)
    stage_a(4)
    stage_z(0, 2)
    stage_z(1, 1)
    stage_b(3)
    stage_s(2)
    stage_z(0, 3)
    stage_c(2)
    stage_s(3)
    stage_z(1, 2)
    stage_b(4)
    stage_z5(0)
    stage_y1(0)
    stage_d(2)
    stage_c(3)
    stage_z(1, 3)
    stage_e(2)
    stage_s(4)
    stage_c(4)
    stage_d(3)
    stage_e(3)
    stage_z(2, 1)
    stage_d(4)
    stage_z(3, 1)
    stage_z5(1)
    stage_y1(1)
    stage_f(3)
    stage_y2(0)
    stage_e(4)
    stage_y2(1)
    stage_q(4)
    stage_f(2)
    stage_y3(0)
    stage_y3(1)
    stage_w(3)
    stage_z(2, 2)
    stage_z(3, 2)
    stage_f(4)
    stage_y4(0)
    stage_w(2)
    stage_z(2, 3)
    stage_z(3, 3)
    stage_y4(1)
    stage_w(4)
    stage_z5(2)
    stage_g(2)
    stage_z5(3)
    stage_g(3)
    stage_g(4)

    used = hid[:, ROWS : ROWS + COUNT_ROWS, 0:128].astype(F32)
    count = jnp.sum(used) * (1.0 / (4 * 128))
    mean_ref[...] = colsum[:, 0:units] / count
    row_mean = gram[:, units : units + 1] / count
    col_mean = colsum[0:1, units:] / count
    cov_ref[...] = gram[:, 0:units] / count - row_mean * col_mean

    for copy in sends:
        copy.wait_send()
    for k in RELAY:
        @pl.when(on_line & (d != 3))
        def _():
            bcopy(hidz, k, 0, True).wait_send()

        @pl.when(on_line & (d != 1))
        def _():
            bcopy(hidz, k, 1, True).wait_send()

        @pl.when(on_line)
        def _():
            bcopy(hidz, k, 0, False).wait_send()
            bcopy(hidz, k, 1, False).wait_send()
    for k in DIRECT:
        for i in (1, 2, 3):
            side_copy(k, i).wait_send()
        for j in range(YS):
            @pl.when(z != block_of(j))
            def _():
                block_copy(k, j).wait_send()

        @pl.when(on_line)
        def _():
            line_copy(k).wait_send()


def local(tokens, routes, slots, gate_weight, up_weight):
    tok_rows, depth = tokens.shape
    units = gate_weight.shape[1]
    hrows = ROWS + COUNT_ROWS
    nk = len(CHUNKS)
    vmem = pl.BlockSpec(memory_space=pltpu.VMEM)
    hbm = pl.BlockSpec(memory_space=pl.ANY)
    dma = pltpu.SemaphoreType.DMA
    cov, means = pl.pallas_call(
        kernel,
        out_shape=(
            jax.ShapeDtypeStruct((units, units), F32),
            jax.ShapeDtypeStruct((8, units), F32),
        ),
        in_specs=[vmem, vmem, vmem, hbm, hbm],
        out_specs=(vmem, vmem),
        scratch_shapes=[
            pltpu.VMEM((XS, CAP, depth + FLAG), BF16),
            pltpu.VMEM((ROWS, depth + FLAG), BF16),
            pltpu.VMEM((depth, units), BF16),
            pltpu.VMEM((depth, units), BF16),
            pltpu.VMEM((ZS, hrows, units), BF16),
            pltpu.VMEM((ZS, hrows, units), BF16),
            pltpu.VMEM((YS - 1, ROWS, units), BF16),
            pltpu.VMEM((units, units + 128), F32),
            pltpu.VMEM((8, 2 * units), F32),
            dma((2,)), dma((nk,)),
            dma((nk,)), dma((nk,)),
            dma((nk, 2, 2)), dma((nk, 2, 2)),
            dma((nk, 2)), dma((nk, 2)),
            dma((nk, 4)), dma((nk, 4)),
            dma((nk, 4, 2)), dma((nk, 4, 2)),
            dma((nk, ZS - 1)), dma((nk, ZS - 1)),
            dma((nk, 2)), dma((nk, 2)), dma((nk, 2)),
            dma((nk, YS - 1)), dma((nk, YS - 1)),
            dma((nk, YS)), dma((nk, ZS)),
            dma((nk,)), dma((nk,)),
        ],
        compiler_params=pltpu.CompilerParams(
            collective_id=0, has_side_effects=True, vmem_limit_bytes=60 << 20
        ),
        name="moments",
    )(tokens, routes.T, slots.T, gate_weight, up_weight)
    return means[0], cov


def solution(mesh):
    in_specs = (
        P(("dp", "expert"), None),
        P(("dp", "expert"), None),
        P(("dp", "expert"), None),
        P(None, "expert"),
        P(None, "expert"),
    )
    out_specs = (P("expert"), P("expert", "dp"))
    return jax.shard_map(local, mesh=mesh, in_specs=in_specs, out_specs=out_specs, check_vma=False)
```

```python
import functools

import jax
import jax.numpy as jnp
from jax import lax
from jax.experimental import pallas as pl
from jax.experimental.pallas import tpu as pltpu
from jax.sharding import PartitionSpec as P

MESH = pl.DeviceIdType.MESH
F32 = jnp.float32
BF16 = jnp.bfloat16

CAP = 16
XS = 4
YS = 4
ZS = 8
FLAG = 128
CHUNKS = ((0, 0, 16, 0), (1, 0, 16, 128), (3, 0, 16, 256), (2, 0, 16, 384))
ROWS = 2 * XS * YS * CAP
COUNT_ROWS = 16


RELAY = (0, 1)
DIRECT = tuple(k for k in range(len(CHUNKS)) if k not in RELAY)
STRAIGHT = ()
PAIRED = ()


def kernel(
    tok_hbm, routes_hbm, slots_hbm, wg_hbm, wu_hbm, cov_ref, mean_ref,
    tok_ref, routes_ref, slots_ref, packed, rows, wg, wu, hid, hidz, hidy, gram, colsum,
    w_sem, l_sem, x_s, x_r, ya_s, ya_r, yb_s, yb_r, sb_s, sb_r,
    z_s, z_r, zd_s, zd_r, h_s, h_r, hs_s, ye_s, ye_r, e_s, e_r, t_s, t_r,
):
    depth = wg.shape[0]
    units = wg.shape[1]
    wide = depth + FLAG
    half = depth // 2
    last = len(CHUNKS) - 1

    z = lax.axis_index("dp")
    member = lax.axis_index("expert")
    x = member // (2 * YS)
    y = (member // 2) % YS
    c = member % 2

    def dev(dx=0, dy=0, dz=0, dc=0):
        xx = (x + dx) % XS
        yy = (y + dy) % YS
        cc = (c + dc) % 2
        return {"dp": (z + dz) % ZS, "expert": (xx * YS + yy) * 2 + cc}

    peers = [dict(dx=1), dict(dx=2), dict(dx=3), dict(dy=1), dict(dy=2), dict(dy=3), dict(dc=1)]
    peers += [dict(dz=s) for s in range(1, ZS)]
    barrier = pltpu.get_barrier_semaphore()
    for p in peers:
        pl.semaphore_signal(barrier, inc=1, device_id=dev(**p), device_id_type=MESH)
    on_line = c == z % 2
    wg_copy = pltpu.make_async_copy(wg_hbm, wg, w_sem.at[0])
    wu_copy = pltpu.make_async_copy(wu_hbm, wu, w_sem.at[1])
    fetches = [
        pltpu.make_async_copy(src, dst, w_sem.at[2 + i])
        for i, (src, dst) in enumerate(((routes_hbm, routes_ref), (slots_hbm, slots_ref), (tok_hbm, tok_ref)))
    ]
    for copy in fetches:
        copy.start()
    wg_copy.start()
    wu_copy.start()
    gram[...] = jnp.zeros_like(gram)
    colsum[...] = jnp.zeros_like(colsum)
    for copy in fetches:
        copy.wait()

    routes = routes_ref[...]
    slots = slots_ref[...]
    usable = (routes < XS) & (slots < CAP)
    target = jnp.where(usable, routes * CAP + slots, -1)
    tok_rows = routes.shape[1]
    places = lax.broadcasted_iota(jnp.int32, (XS * CAP, tok_rows), 0)
    hit = jnp.zeros((XS * CAP, tok_rows), F32)
    for k in range(routes.shape[0]):
        hit = jnp.maximum(hit, jnp.where(target[k : k + 1, :] == places, 1.0, 0.0))
    placing = hit.astype(BF16)

    def tdot(a, b):
        return lax.dot_general(a, b, (((0,), (0,)), ((), ())), preferred_element_type=F32)

    step = depth // 7
    for j in range(7):
        part = jnp.dot(placing, tok_ref[:, j * step : (j + 1) * step], preferred_element_type=F32).astype(BF16)
        for g in range(XS):
            packed[g, :, j * step : (j + 1) * step] = part[g * CAP : (g + 1) * CAP]
    flags = jnp.dot(placing, jnp.ones((tok_rows, FLAG), BF16), preferred_element_type=F32).astype(BF16)
    for g in range(XS):
        packed[g, :, depth:wide] = flags[g * CAP : (g + 1) * CAP]

    pl.semaphore_wait(barrier, len(peers))

    sends = []

    def send(src, dst, ss, rs, to):
        copy = pltpu.make_async_remote_copy(
            src_ref=src, dst_ref=dst, send_sem=ss, recv_sem=rs, device_id=to, device_id_type=MESH
        )
        copy.start()
        return copy

    def arrived(dst, rs):
        pltpu.make_async_remote_copy(
            src_ref=dst, dst_ref=dst, send_sem=rs, recv_sem=rs, device_id=dev(dc=1), device_id_type=MESH
        ).wait_recv()

    def size(k):
        return 2 * YS * CHUNKS[k][2]

    def piece_rows(k, yy, cc):
        n = CHUNKS[k][2]
        return pl.ds(pl.multiple_of(CHUNKS[k][3] + (yy * 2 + cc) * n, n), n)

    def lanes(h):
        return pl.ds(0, half) if h == 0 else pl.ds(half, wide - half)

    def piece(k, yy, cc):
        return rows.at[piece_rows(k, yy, cc), :]

    def half_piece(k, yy, cc, h):
        return rows.at[piece_rows(k, yy, cc), lanes(h)]

    y_up, y_dn, y_op = (y + 1) % YS, (y + YS - 1) % YS, (y + 2) % YS

    def stage_a(k):
        dx, lo, n, _ = CHUNKS[k]
        if dx == 0:
            own = packed.at[x, pl.ds(lo, n), :]
        else:
            own = piece(k, y, c)
            arrived(own, x_r.at[k])
        for i in range(2):
            for way in range(2):
                h = way if i == 0 else 1 - way
                src = packed.at[x, pl.ds(lo, n), lanes(h)] if dx == 0 else half_piece(k, y, c, h)
                to = dev(dy=1 if way == 0 else 3)
                sends.append(send(src, half_piece(k, y, c, h), ya_s.at[k, way, i], ya_r.at[k, way, i], to))
        sends.append(send(own, piece(k, y, c), sb_s.at[k, 0], sb_r.at[k, 0], dev(dc=1)))

    def stage_b(k):
        for way, yy in enumerate((y_dn, y_up)):
            part = half_piece(k, yy, c, way)
            arrived(part, ya_r.at[k, way, 0])
            sends.append(send(part, part, yb_s.at[k, way], yb_r.at[k, way], dev(dy=1 if way == 0 else 3)))

    def stage_s(k):
        for way, yy in enumerate((y_dn, y_up)):
            arrived(half_piece(k, yy, c, 1 - way), ya_r.at[k, way, 1])
            sends.append(send(piece(k, yy, c), piece(k, yy, c), sb_s.at[k, 1 + way], sb_r.at[k, 1 + way], dev(dc=1)))

    def stage_c(k):
        arrived(half_piece(k, y_op, c, 0), yb_r.at[k, 0])
        arrived(half_piece(k, y_op, c, 1), yb_r.at[k, 1])
        sends.append(send(piece(k, y_op, c), piece(k, y_op, c), sb_s.at[k, 3], sb_r.at[k, 3], dev(dc=1)))

    def hrows(k):
        return pl.ds(CHUNKS[k][3], size(k) + (COUNT_ROWS if k == last else 0))

    def hslot(k, s):
        return hid.at[s, hrows(k), :]

    def hhalf(k, s, h):
        n = size(k) // 2
        return hid.at[s, pl.ds(CHUNKS[k][3] + h * n, n + (COUNT_ROWS if k == last and h == 1 else 0)), :]

    def stage_d(k):
        for i, yy in enumerate((y, y_dn, y_up, y_op)):
            arrived(piece(k, yy, (c + 1) % 2), sb_r.at[k, i])
        if k == 0:
            wg_copy.wait()
            wu_copy.wait()
        at, n = CHUNKS[k][3], size(k)
        lhs = rows[at : at + n, 0:depth]
        gate = jnp.dot(lhs, wg[...], preferred_element_type=F32)
        up = jnp.dot(lhs, wu[...], preferred_element_type=F32)
        hid[0, at : at + n, :] = (gate / (1.0 + jnp.exp(-gate)) * up).astype(BF16)
        if k == last:
            for r in range(4):
                part = ROWS // 4
                used = jnp.sum(rows[r * part : (r + 1) * part, depth:wide].astype(F32), axis=0, keepdims=True)
                used = jnp.concatenate([used, used], axis=1)
                hid[0, ROWS + 4 * r : ROWS + 4 * (r + 1), :] = jnp.broadcast_to(used, (4, units)).astype(BF16)
        if k in STRAIGHT:
            for s in (4, 3, 5, 2, 6, 1, 7):
                sends.append(send(hslot(k, 0), hslot(k, s), zd_s.at[k, s - 1], zd_r.at[k, s - 1], dev(dz=s)))
        elif k in PAIRED:
            for way, (near, far) in enumerate(((1, 2), (7, 6))):
                sends.append(send(hslot(k, 0), hslot(k, far), z_s.at[k, 1, way], z_r.at[k, 1, way], dev(dz=far)))
                sends.append(send(hslot(k, 0), hslot(k, near), z_s.at[k, 0, way], z_r.at[k, 0, way], dev(dz=near)))
        else:
            sends.append(send(hslot(k, 0), hslot(k, 1), z_s.at[k, 0, 0], z_r.at[k, 0, 0], dev(dz=1)))
            sends.append(send(hslot(k, 0), hslot(k, 7), z_s.at[k, 0, 1], z_r.at[k, 0, 1], dev(dz=7)))

    def stage_q(k):
        for s in range(1, ZS):
            arrived(hslot(k, s), zd_r.at[k, s - 1])

    def stage_p(k):
        for way, (near, far, third) in enumerate(((1, 2, 3), (7, 6, 5))):
            arrived(hslot(k, far), z_r.at[k, 1, way])
            sends.append(send(hslot(k, far), hslot(k, third), z_s.at[k, 2, way], z_r.at[k, 2, way], dev(dz=near)))
            sends.append(send(hhalf(k, far, way), hhalf(k, 4, way), z_s.at[k, 3, way], z_r.at[k, 3, way], dev(dz=far)))

    def stage_z(k, t):
        arrived(hslot(k, t), z_r.at[k, t - 1, 0])
        if t < 3:
            sends.append(send(hslot(k, t), hslot(k, t + 1), z_s.at[k, t, 0], z_r.at[k, t, 0], dev(dz=1)))
        else:
            sends.append(send(hhalf(k, 3, 0), hhalf(k, 4, 0), z_s.at[k, 3, 0], z_r.at[k, 3, 0], dev(dz=1)))
        arrived(hslot(k, 8 - t), z_r.at[k, t - 1, 1])
        if t < 3:
            sends.append(send(hslot(k, 8 - t), hslot(k, 7 - t), z_s.at[k, t, 1], z_r.at[k, t, 1], dev(dz=7)))
        else:
            sends.append(send(hhalf(k, 5, 1), hhalf(k, 4, 1), z_s.at[k, 3, 1], z_r.at[k, 3, 1], dev(dz=7)))

    def stage_z5(k):
        if k in PAIRED:
            for way, (near, third) in enumerate(((1, 3), (7, 5))):
                arrived(hslot(k, near), z_r.at[k, 0, way])
                arrived(hslot(k, third), z_r.at[k, 2, way])
        arrived(hhalf(k, 4, 0), z_r.at[k, 3, 0])
        arrived(hhalf(k, 4, 1), z_r.at[k, 3, 1])

    def accumulate(k):
        at, n = CHUNKS[k][3], ZS * size(k)
        a = hid[:, at : at + size(k), :].reshape(n, units)
        b = hidz[:, at : at + size(k), :].reshape(n, units)
        ones_l = jnp.ones((n, 128), BF16)
        ones_s = jnp.ones((8, n), BF16)
        gram[...] += tdot(a, jnp.concatenate([b, ones_l], axis=1))
        colsum[...] += jnp.dot(ones_s, jnp.concatenate([a, b], axis=1), preferred_element_type=F32)

    d = (y + YS - z // 2) % YS

    def bpart(ref, k, h):
        return ref.at[pl.ds(4 * h, 4), pl.ds(CHUNKS[k][3], size(k)), :]

    def bcopy(src, k, h, to_y):
        if to_y:
            ss, to = h_s.at[k, h], dev(dy=1 if h == 0 else 3)
        else:
            ss, to = hs_s.at[k, h], dev(dc=1)
        return pltpu.make_async_remote_copy(
            src_ref=bpart(src, k, h), dst_ref=bpart(hidz, k, h), send_sem=ss, recv_sem=h_r.at[k, h],
            device_id=to, device_id_type=MESH,
        )

    def own_copy(k):
        return pltpu.make_async_copy(
            hid.at[:, pl.ds(CHUNKS[k][3], size(k)), :], hidz.at[:, pl.ds(CHUNKS[k][3], size(k)), :], l_sem.at[k]
        )

    def bforward(k, h, to_y):
        arrived(bpart(hidz, k, h), h_r.at[k, h])
        if to_y:
            bcopy(hidz, k, h, True).start()
        bcopy(hidz, k, h, False).start()

    def stage_y1(k):
        @pl.when(on_line & (d == 0))
        def _():
            for h in range(2):
                bcopy(hid, k, h, True).start()
            for h in range(2):
                bcopy(hid, k, h, False).start()
            own_copy(k).start()

    def stage_y2(k):
        @pl.when(on_line & (d == 1))
        def _():
            bforward(k, 0, True)

        @pl.when(on_line & (d == 3))
        def _():
            bforward(k, 1, True)

    def stage_y3(k):
        @pl.when(on_line & (d == 2))
        def _():
            bforward(k, 0, True)
            bforward(k, 1, True)

    def stage_y4(k):
        @pl.when(on_line & (d == 1))
        def _():
            bforward(k, 1, False)

        @pl.when(on_line & (d == 3))
        def _():
            bforward(k, 0, False)

        @pl.when(on_line & (d == 0))
        def _():
            own_copy(k).wait()

        @pl.when(jnp.logical_not(on_line))
        def _():
            arrived(bpart(hidz, k, 0), h_r.at[k, 0])
            arrived(bpart(hidz, k, 1), h_r.at[k, 1])

        accumulate(k)

    def krows(ref, k, s):
        return ref.at[s, pl.ds(CHUNKS[k][3], size(k)), :]

    def block_of(j):
        return 2 * ((y + j) % YS) + c

    def held(k, j):
        return krows(hid, k, 0) if j == 0 else krows(hidy, k, j - 1)

    def side_copy(k, i):
        return pltpu.make_async_remote_copy(
            src_ref=krows(hid, k, 0), dst_ref=krows(hidy, k, YS - i - 1), send_sem=ye_s.at[k, i - 1],
            recv_sem=ye_r.at[k, YS - i - 1], device_id=dev(dy=i), device_id_type=MESH,
        )

    def block_copy(k, j):
        block = block_of(j)
        slot = (block + ZS - z) % ZS
        return pltpu.make_async_remote_copy(
            src_ref=held(k, j), dst_ref=krows(hidz, k, slot), send_sem=e_s.at[k, j],
            recv_sem=e_r.at[k, slot], device_id={"dp": block, "expert": member}, device_id_type=MESH,
        )

    def kept_copy(k, j):
        return pltpu.make_async_copy(held(k, j), krows(hidz, k, 0), l_sem.at[k])

    def line_copy(k):
        part = hidz.at[:, pl.ds(CHUNKS[k][3], size(k)), :]
        return pltpu.make_async_remote_copy(
            src_ref=part, dst_ref=part, send_sem=t_s.at[k], recv_sem=t_r.at[k],
            device_id=dev(dc=1), device_id_type=MESH,
        )

    def pass_on(k, j):
        if j > 0:
            arrived(held(k, j), ye_r.at[k, j - 1])

        @pl.when(z == block_of(j))
        def _():
            kept_copy(k, j).start()

        @pl.when(z != block_of(j))
        def _():
            block_copy(k, j).start()

    def stage_e(k):
        for i in (1, 3, 2):
            side_copy(k, i).start()
        pass_on(k, 0)

    def stage_f(k):
        for j in (1, 3, 2):
            pass_on(k, j)

    def stage_w(k):
        @pl.when(on_line)
        def _():
            for s in range(1, ZS):
                arrived(krows(hidz, k, s), e_r.at[k, s])
            kept_copy(k, 0).wait()
            line_copy(k).start()

    def stage_g(k):
        @pl.when(jnp.logical_not(on_line))
        def _():
            line_copy(k).wait_recv()

        accumulate(k)

    def sent_y(k):
        @pl.when(on_line & (d != 3))
        def _():
            bcopy(hidz, k, 0, True).wait_send()

        @pl.when(on_line & (d != 1))
        def _():
            bcopy(hidz, k, 1, True).wait_send()

        @pl.when(on_line)
        def _():
            bcopy(hidz, k, 0, False).wait_send()
            bcopy(hidz, k, 1, False).wait_send()

    def sent_e(k):
        for i in (1, 2, 3):
            side_copy(k, i).wait_send()
        for j in range(YS):
            @pl.when(z != block_of(j))
            def _():
                block_copy(k, j).wait_send()

        @pl.when(on_line)
        def _():
            line_copy(k).wait_send()

    def flush():
        while sends:
            sends.pop().wait_send()

    stage_a(0)
    for k, (dx, lo, n, _) in enumerate(CHUNKS):
        if dx > 0:
            src = packed.at[(x + dx) % XS, pl.ds(lo, n), :]
            sends.append(send(src, piece(k, y, c), x_s.at[k], x_r.at[k], dev(dx=dx)))
        else:
            rows[piece_rows(k, y, c), :] = packed[x, lo : lo + n]

    stage_b(0)
    stage_a(1)
    stage_c(0)
    stage_b(1)
    stage_s(0)
    stage_a(2)
    stage_d(0)
    stage_s(1)
    stage_c(1)
    stage_z(0, 1)
    stage_b(2)
    stage_d(1)
    stage_a(3)
    stage_z(0, 2)
    stage_s(2)
    stage_c(2)
    stage_z(1, 1)
    stage_z(0, 3)
    stage_b(3)
    stage_d(2)
    stage_z5(0)
    stage_y1(0)
    stage_e(2)
    stage_s(3)
    stage_z(1, 2)
    stage_c(3)
    stage_z(2, 1)
    stage_z(1, 3)
    stage_y2(0)
    stage_d(3)
    stage_z5(1)
    stage_f(2)
    stage_y1(1)
    stage_e(3)
    stage_y2(1)
    stage_z(3, 1)
    stage_y3(0)
    stage_z(2, 2)
    stage_f(3)
    stage_w(2)
    stage_y3(1)
    stage_z(2, 3)
    stage_z(3, 2)
    stage_y4(0)
    stage_z5(2)
    stage_w(3)
    stage_g(2)
    stage_z(3, 3)
    flush()
    stage_y4(1)
    stage_z5(3)
    stage_g(3)

    used = hid[:, ROWS : ROWS + COUNT_ROWS, 0:128].astype(F32)
    count = jnp.sum(used) * (1.0 / (4 * 128))
    mean_ref[...] = colsum[0:1, 0:units] / count
    row_mean = gram[:, units : units + 1] / count
    col_mean = colsum[0:1, units:] / count
    cov_ref[...] = gram[:, 0:units] / count - row_mean * col_mean

    flush()
    for k in RELAY:
        sent_y(k)
    for k in DIRECT:
        sent_e(k)


def local(tokens, routes, slots, gate_weight, up_weight):
    tok_rows, depth = tokens.shape
    units = gate_weight.shape[1]
    hrows = ROWS + COUNT_ROWS
    nk = len(CHUNKS)
    vmem = pl.BlockSpec(memory_space=pltpu.VMEM)
    hbm = pl.BlockSpec(memory_space=pl.ANY)
    dma = pltpu.SemaphoreType.DMA
    cov, means = pl.pallas_call(
        kernel,
        out_shape=(
            jax.ShapeDtypeStruct((units, units), F32),
            jax.ShapeDtypeStruct((1, units), F32),
        ),
        in_specs=[hbm, hbm, hbm, hbm, hbm],
        out_specs=(vmem, vmem),
        scratch_shapes=[
            pltpu.VMEM(tokens.shape, BF16),
            pltpu.VMEM(routes.shape[::-1], jnp.int32),
            pltpu.VMEM(routes.shape[::-1], jnp.int32),
            pltpu.VMEM((XS, CAP, depth + FLAG), BF16),
            pltpu.VMEM((ROWS, depth + FLAG), BF16),
            pltpu.VMEM((depth, units), BF16),
            pltpu.VMEM((depth, units), BF16),
            pltpu.VMEM((ZS, hrows, units), BF16),
            pltpu.VMEM((ZS, hrows, units), BF16),
            pltpu.VMEM((YS - 1, ROWS, units), BF16),
            pltpu.VMEM((units, units + 128), F32),
            pltpu.VMEM((8, 2 * units), F32),
            dma((5,)), dma((nk,)),
            dma((nk,)), dma((nk,)),
            dma((nk, 2, 2)), dma((nk, 2, 2)),
            dma((nk, 2)), dma((nk, 2)),
            dma((nk, 4)), dma((nk, 4)),
            dma((nk, 4, 2)), dma((nk, 4, 2)),
            dma((nk, ZS - 1)), dma((nk, ZS - 1)),
            dma((nk, 2)), dma((nk, 2)), dma((nk, 2)),
            dma((nk, YS - 1)), dma((nk, YS - 1)),
            dma((nk, YS)), dma((nk, ZS)),
            dma((nk,)), dma((nk,)),
        ],
        compiler_params=pltpu.CompilerParams(
            collective_id=0, has_side_effects=True, vmem_limit_bytes=60 << 20
        ),
        name="moments",
    )(tokens, routes.T, slots.T, gate_weight, up_weight)
    return means.reshape(units), cov


def solution(mesh):
    in_specs = (
        P(("dp", "expert"), None),
        P(("dp", "expert"), None),
        P(("dp", "expert"), None),
        P(None, "expert"),
        P(None, "expert"),
    )
    out_specs = (P("expert"), P("expert", "dp"))
    return jax.shard_map(local, mesh=mesh, in_specs=in_specs, out_specs=out_specs, check_vma=False)
```

```python
import functools

import jax
import jax.numpy as jnp
from jax import lax
from jax.experimental import pallas as pl
from jax.experimental.pallas import tpu as pltpu
from jax.sharding import PartitionSpec as P

MESH = pl.DeviceIdType.MESH
F32 = jnp.float32
BF16 = jnp.bfloat16

CAP = 16
XS = 4
YS = 4
ZS = 8
FLAG = 128
CHUNKS = ((0, 0, 16, 0), (1, 0, 16, 128), (3, 0, 16, 256), (2, 0, 16, 384))
ROWS = 2 * XS * YS * CAP
COUNT_ROWS = 16


RELAY = (0, 1)
DIRECT = tuple(k for k in range(len(CHUNKS)) if k not in RELAY)
STRAIGHT = ()
PAIRED = ()


def kernel(
    tok_hbm, routes_hbm, slots_hbm, wg_hbm, wu_hbm, cov_ref, mean_ref,
    tok_ref, routes_ref, slots_ref, packed, rows, wg, wu, hid, hidz, hidy, gram, colsum,
    w_sem, l_sem, x_s, x_r, ya_s, ya_r, yb_s, yb_r, sb_s, sb_r,
    z_s, z_r, zd_s, zd_r, h_s, h_r, hs_s, ye_s, ye_r, e_s, e_r, t_s, t_r,
):
    depth = wg.shape[0]
    units = wg.shape[1]
    wide = depth + FLAG
    half = depth // 2
    last = len(CHUNKS) - 1

    z = lax.axis_index("dp")
    member = lax.axis_index("expert")
    x = member // (2 * YS)
    y = (member // 2) % YS
    c = member % 2

    def dev(dx=0, dy=0, dz=0, dc=0):
        xx = (x + dx) % XS
        yy = (y + dy) % YS
        cc = (c + dc) % 2
        return {"dp": (z + dz) % ZS, "expert": (xx * YS + yy) * 2 + cc}

    peers = [dict(dx=1), dict(dx=2), dict(dx=3), dict(dy=1), dict(dy=2), dict(dy=3), dict(dc=1)]
    peers += [dict(dz=s) for s in range(1, ZS)]
    barrier = pltpu.get_barrier_semaphore()
    for p in peers:
        pl.semaphore_signal(barrier, inc=1, device_id=dev(**p), device_id_type=MESH)
    on_line = c == z % 2
    wg_copy = pltpu.make_async_copy(wg_hbm, wg, w_sem.at[0])
    wu_copy = pltpu.make_async_copy(wu_hbm, wu, w_sem.at[1])
    fetches = [
        pltpu.make_async_copy(src, dst, w_sem.at[2 + i])
        for i, (src, dst) in enumerate(((routes_hbm, routes_ref), (slots_hbm, slots_ref), (tok_hbm, tok_ref)))
    ]
    for copy in fetches:
        copy.start()
    wg_copy.start()
    wu_copy.start()
    gram[...] = jnp.zeros_like(gram)
    colsum[...] = jnp.zeros_like(colsum)
    for copy in fetches:
        copy.wait()

    routes = routes_ref[...]
    slots = slots_ref[...]
    usable = (routes < XS) & (slots < CAP)
    target = jnp.where(usable, routes * CAP + slots, -1)
    tok_rows = routes.shape[1]
    places = lax.broadcasted_iota(jnp.int32, (XS * CAP, tok_rows), 0)
    hit = jnp.zeros((XS * CAP, tok_rows), F32)
    for k in range(routes.shape[0]):
        hit = jnp.maximum(hit, jnp.where(target[k : k + 1, :] == places, 1.0, 0.0))
    placing = hit.astype(BF16)

    def tdot(a, b):
        return lax.dot_general(a, b, (((0,), (0,)), ((), ())), preferred_element_type=F32)

    step = depth // 7
    for j in range(7):
        part = jnp.dot(placing, tok_ref[:, j * step : (j + 1) * step], preferred_element_type=F32).astype(BF16)
        for g in range(XS):
            packed[g, :, j * step : (j + 1) * step] = part[g * CAP : (g + 1) * CAP]
    flags = jnp.dot(placing, jnp.ones((tok_rows, FLAG), BF16), preferred_element_type=F32).astype(BF16)
    for g in range(XS):
        packed[g, :, depth:wide] = flags[g * CAP : (g + 1) * CAP]

    pl.semaphore_wait(barrier, len(peers))

    sends = []

    def send(src, dst, ss, rs, to):
        copy = pltpu.make_async_remote_copy(
            src_ref=src, dst_ref=dst, send_sem=ss, recv_sem=rs, device_id=to, device_id_type=MESH
        )
        copy.start()
        return copy

    def arrived(dst, rs):
        pltpu.make_async_remote_copy(
            src_ref=dst, dst_ref=dst, send_sem=rs, recv_sem=rs, device_id=dev(dc=1), device_id_type=MESH
        ).wait_recv()

    def size(k):
        return 2 * YS * CHUNKS[k][2]

    def piece_rows(k, yy, cc):
        n = CHUNKS[k][2]
        return pl.ds(pl.multiple_of(CHUNKS[k][3] + (yy * 2 + cc) * n, n), n)

    def lanes(h):
        return pl.ds(0, half) if h == 0 else pl.ds(half, wide - half)

    def piece(k, yy, cc):
        return rows.at[piece_rows(k, yy, cc), :]

    def half_piece(k, yy, cc, h):
        return rows.at[piece_rows(k, yy, cc), lanes(h)]

    y_up, y_dn, y_op = (y + 1) % YS, (y + YS - 1) % YS, (y + 2) % YS

    def stage_a(k):
        dx, lo, n, _ = CHUNKS[k]
        if dx == 0:
            own = packed.at[x, pl.ds(lo, n), :]
        else:
            own = piece(k, y, c)
            arrived(own, x_r.at[k])
        for i in range(2):
            for way in range(2):
                h = way if i == 0 else 1 - way
                src = packed.at[x, pl.ds(lo, n), lanes(h)] if dx == 0 else half_piece(k, y, c, h)
                to = dev(dy=1 if way == 0 else 3)
                sends.append(send(src, half_piece(k, y, c, h), ya_s.at[k, way, i], ya_r.at[k, way, i], to))
        sends.append(send(own, piece(k, y, c), sb_s.at[k, 0], sb_r.at[k, 0], dev(dc=1)))

    def stage_b(k):
        for way, yy in enumerate((y_dn, y_up)):
            part = half_piece(k, yy, c, way)
            arrived(part, ya_r.at[k, way, 0])
            sends.append(send(part, part, yb_s.at[k, way], yb_r.at[k, way], dev(dy=1 if way == 0 else 3)))

    def stage_s(k):
        for way, yy in enumerate((y_dn, y_up)):
            arrived(half_piece(k, yy, c, 1 - way), ya_r.at[k, way, 1])
            sends.append(send(piece(k, yy, c), piece(k, yy, c), sb_s.at[k, 1 + way], sb_r.at[k, 1 + way], dev(dc=1)))

    def stage_c(k):
        arrived(half_piece(k, y_op, c, 0), yb_r.at[k, 0])
        arrived(half_piece(k, y_op, c, 1), yb_r.at[k, 1])
        sends.append(send(piece(k, y_op, c), piece(k, y_op, c), sb_s.at[k, 3], sb_r.at[k, 3], dev(dc=1)))

    def hrows(k):
        return pl.ds(CHUNKS[k][3], size(k) + (COUNT_ROWS if k == last else 0))

    def hslot(k, s):
        return hid.at[s, hrows(k), :]

    def hhalf(k, s, h):
        n = size(k) // 2
        return hid.at[s, pl.ds(CHUNKS[k][3] + h * n, n + (COUNT_ROWS if k == last and h == 1 else 0)), :]

    def stage_d(k):
        for i, yy in enumerate((y, y_dn, y_up, y_op)):
            arrived(piece(k, yy, (c + 1) % 2), sb_r.at[k, i])
        if k == 0:
            wg_copy.wait()
            wu_copy.wait()
        at, n = CHUNKS[k][3], size(k)
        lhs = rows[at : at + n, 0:depth]
        gate = jnp.dot(lhs, wg[...], preferred_element_type=F32)
        up = jnp.dot(lhs, wu[...], preferred_element_type=F32)
        hid[0, at : at + n, :] = (gate / (1.0 + jnp.exp(-gate)) * up).astype(BF16)
        used = jnp.sum(rows[at : at + n, depth:wide].astype(F32), axis=0, keepdims=True)
        used = jnp.concatenate([used, used], axis=1)
        hid[0, ROWS + 4 * k : ROWS + 4 * (k + 1), :] = jnp.broadcast_to(used, (4, units)).astype(BF16)
        if k in STRAIGHT:
            for s in (4, 3, 5, 2, 6, 1, 7):
                sends.append(send(hslot(k, 0), hslot(k, s), zd_s.at[k, s - 1], zd_r.at[k, s - 1], dev(dz=s)))
        elif k in PAIRED:
            for way, (near, far) in enumerate(((1, 2), (7, 6))):
                sends.append(send(hslot(k, 0), hslot(k, far), z_s.at[k, 1, way], z_r.at[k, 1, way], dev(dz=far)))
                sends.append(send(hslot(k, 0), hslot(k, near), z_s.at[k, 0, way], z_r.at[k, 0, way], dev(dz=near)))
        else:
            sends.append(send(hslot(k, 0), hslot(k, 1), z_s.at[k, 0, 0], z_r.at[k, 0, 0], dev(dz=1)))
            sends.append(send(hslot(k, 0), hslot(k, 7), z_s.at[k, 0, 1], z_r.at[k, 0, 1], dev(dz=7)))

    def stage_q(k):
        for s in range(1, ZS):
            arrived(hslot(k, s), zd_r.at[k, s - 1])

    def stage_p(k):
        for way, (near, far, third) in enumerate(((1, 2, 3), (7, 6, 5))):
            arrived(hslot(k, far), z_r.at[k, 1, way])
            sends.append(send(hslot(k, far), hslot(k, third), z_s.at[k, 2, way], z_r.at[k, 2, way], dev(dz=near)))
            sends.append(send(hhalf(k, far, way), hhalf(k, 4, way), z_s.at[k, 3, way], z_r.at[k, 3, way], dev(dz=far)))

    def stage_z(k, t):
        arrived(hslot(k, t), z_r.at[k, t - 1, 0])
        if t < 3:
            sends.append(send(hslot(k, t), hslot(k, t + 1), z_s.at[k, t, 0], z_r.at[k, t, 0], dev(dz=1)))
        else:
            sends.append(send(hhalf(k, 3, 0), hhalf(k, 4, 0), z_s.at[k, 3, 0], z_r.at[k, 3, 0], dev(dz=1)))
        arrived(hslot(k, 8 - t), z_r.at[k, t - 1, 1])
        if t < 3:
            sends.append(send(hslot(k, 8 - t), hslot(k, 7 - t), z_s.at[k, t, 1], z_r.at[k, t, 1], dev(dz=7)))
        else:
            sends.append(send(hhalf(k, 5, 1), hhalf(k, 4, 1), z_s.at[k, 3, 1], z_r.at[k, 3, 1], dev(dz=7)))

    def stage_z5(k):
        if k in PAIRED:
            for way, (near, third) in enumerate(((1, 3), (7, 5))):
                arrived(hslot(k, near), z_r.at[k, 0, way])
                arrived(hslot(k, third), z_r.at[k, 2, way])
        arrived(hhalf(k, 4, 0), z_r.at[k, 3, 0])
        arrived(hhalf(k, 4, 1), z_r.at[k, 3, 1])

    def accumulate(k):
        at, n = CHUNKS[k][3], ZS * size(k)
        a = hid[:, at : at + size(k), :].reshape(n, units)
        b = hidz[:, at : at + size(k), :].reshape(n, units)
        ones_l = jnp.ones((n, 128), BF16)
        ones_s = jnp.ones((8, n), BF16)
        gram[...] += tdot(a, jnp.concatenate([b, ones_l], axis=1))
        colsum[...] += jnp.dot(ones_s, jnp.concatenate([a, b], axis=1), preferred_element_type=F32)

    d = (y + YS - z // 2) % YS

    def bpart(ref, k, h):
        return ref.at[pl.ds(4 * h, 4), pl.ds(CHUNKS[k][3], size(k)), :]

    def bcopy(src, k, h, to_y):
        if to_y:
            ss, to = h_s.at[k, h], dev(dy=1 if h == 0 else 3)
        else:
            ss, to = hs_s.at[k, h], dev(dc=1)
        return pltpu.make_async_remote_copy(
            src_ref=bpart(src, k, h), dst_ref=bpart(hidz, k, h), send_sem=ss, recv_sem=h_r.at[k, h],
            device_id=to, device_id_type=MESH,
        )

    def own_copy(k):
        return pltpu.make_async_copy(
            hid.at[:, pl.ds(CHUNKS[k][3], size(k)), :], hidz.at[:, pl.ds(CHUNKS[k][3], size(k)), :], l_sem.at[k]
        )

    def bforward(k, h, to_y):
        arrived(bpart(hidz, k, h), h_r.at[k, h])
        if to_y:
            bcopy(hidz, k, h, True).start()
        bcopy(hidz, k, h, False).start()

    def stage_y1(k):
        @pl.when(on_line & (d == 0))
        def _():
            for h in range(2):
                bcopy(hid, k, h, True).start()
            for h in range(2):
                bcopy(hid, k, h, False).start()
            own_copy(k).start()

    def stage_y2(k):
        @pl.when(on_line & (d == 1))
        def _():
            bforward(k, 0, True)

        @pl.when(on_line & (d == 3))
        def _():
            bforward(k, 1, True)

    def stage_y3(k):
        @pl.when(on_line & (d == 2))
        def _():
            bforward(k, 0, True)
            bforward(k, 1, True)

    def stage_y4(k):
        @pl.when(on_line & (d == 1))
        def _():
            bforward(k, 1, False)

        @pl.when(on_line & (d == 3))
        def _():
            bforward(k, 0, False)

        @pl.when(on_line & (d == 0))
        def _():
            own_copy(k).wait()

        @pl.when(jnp.logical_not(on_line))
        def _():
            arrived(bpart(hidz, k, 0), h_r.at[k, 0])
            arrived(bpart(hidz, k, 1), h_r.at[k, 1])

        accumulate(k)

    def krows(ref, k, s):
        return ref.at[s, pl.ds(CHUNKS[k][3], size(k)), :]

    def block_of(j):
        return 2 * ((y + j) % YS) + c

    def held(k, j):
        return krows(hid, k, 0) if j == 0 else krows(hidy, k, j - 1)

    def side_copy(k, i):
        return pltpu.make_async_remote_copy(
            src_ref=krows(hid, k, 0), dst_ref=krows(hidy, k, YS - i - 1), send_sem=ye_s.at[k, i - 1],
            recv_sem=ye_r.at[k, YS - i - 1], device_id=dev(dy=i), device_id_type=MESH,
        )

    def block_copy(k, j):
        block = block_of(j)
        slot = (block + ZS - z) % ZS
        return pltpu.make_async_remote_copy(
            src_ref=held(k, j), dst_ref=krows(hidz, k, slot), send_sem=e_s.at[k, j],
            recv_sem=e_r.at[k, slot], device_id={"dp": block, "expert": member}, device_id_type=MESH,
        )

    def kept_copy(k, j):
        return pltpu.make_async_copy(held(k, j), krows(hidz, k, 0), l_sem.at[k])

    def line_copy(k):
        part = hidz.at[:, pl.ds(CHUNKS[k][3], size(k)), :]
        return pltpu.make_async_remote_copy(
            src_ref=part, dst_ref=part, send_sem=t_s.at[k], recv_sem=t_r.at[k],
            device_id=dev(dc=1), device_id_type=MESH,
        )

    def pass_on(k, j):
        if j > 0:
            arrived(held(k, j), ye_r.at[k, j - 1])

        @pl.when(z == block_of(j))
        def _():
            kept_copy(k, j).start()

        @pl.when(z != block_of(j))
        def _():
            block_copy(k, j).start()

    def stage_e(k):
        for i in (2, 1, 3):
            side_copy(k, i).start()
        pass_on(k, 0)

    def stage_f(k):
        for j in (1, 3, 2):
            pass_on(k, j)

    def stage_w(k):
        @pl.when(on_line)
        def _():
            for s in range(1, ZS):
                arrived(krows(hidz, k, s), e_r.at[k, s])
            kept_copy(k, 0).wait()
            line_copy(k).start()

    def stage_g(k):
        @pl.when(jnp.logical_not(on_line))
        def _():
            line_copy(k).wait_recv()

        accumulate(k)

    def sent_y(k):
        @pl.when(on_line & (d != 3))
        def _():
            bcopy(hidz, k, 0, True).wait_send()

        @pl.when(on_line & (d != 1))
        def _():
            bcopy(hidz, k, 1, True).wait_send()

        @pl.when(on_line)
        def _():
            bcopy(hidz, k, 0, False).wait_send()
            bcopy(hidz, k, 1, False).wait_send()

    def sent_e(k):
        for i in (1, 2, 3):
            side_copy(k, i).wait_send()
        for j in range(YS):
            @pl.when(z != block_of(j))
            def _():
                block_copy(k, j).wait_send()

        @pl.when(on_line)
        def _():
            line_copy(k).wait_send()

    def flush():
        while sends:
            sends.pop().wait_send()

    stage_a(0)
    for k, (dx, lo, n, _) in enumerate(CHUNKS):
        if dx > 0:
            src = packed.at[(x + dx) % XS, pl.ds(lo, n), :]
            sends.append(send(src, piece(k, y, c), x_s.at[k], x_r.at[k], dev(dx=dx)))
        else:
            rows[piece_rows(k, y, c), :] = packed[x, lo : lo + n]

    stage_b(0)
    stage_a(1)
    stage_c(0)
    stage_b(1)
    stage_s(0)
    stage_a(2)
    stage_d(0)
    stage_s(1)
    stage_c(1)
    stage_z(0, 1)
    stage_b(2)
    stage_d(1)
    stage_a(3)
    stage_z(0, 2)
    stage_s(2)
    stage_c(2)
    stage_z(1, 1)
    stage_z(0, 3)
    stage_b(3)
    stage_d(2)
    stage_z5(0)
    stage_y1(0)
    stage_e(2)
    stage_s(3)
    stage_z(1, 2)
    stage_c(3)
    stage_z(2, 1)
    stage_z(1, 3)
    stage_y2(0)
    stage_d(3)
    stage_e(3)
    stage_z5(1)
    stage_y1(1)
    stage_f(2)
    stage_z(3, 1)
    stage_z(2, 2)
    stage_f(3)
    stage_y2(1)
    stage_y3(0)
    stage_w(2)
    stage_z(3, 2)
    stage_y3(1)
    stage_z(2, 3)
    stage_y4(0)
    stage_z5(2)
    stage_z(3, 3)
    stage_g(2)
    flush()
    stage_w(3)
    stage_y4(1)
    stage_z5(3)
    stage_g(3)

    used = hid[:, ROWS : ROWS + COUNT_ROWS, 0:128].astype(F32)
    count = jnp.sum(used) * (1.0 / (4 * 128))
    mean_ref[...] = colsum[0:1, 0:units] / count
    row_mean = gram[:, units : units + 1] / count
    col_mean = colsum[0:1, units:] / count
    cov_ref[...] = gram[:, 0:units] / count - row_mean * col_mean

    flush()
    for k in RELAY:
        sent_y(k)
    for k in DIRECT:
        sent_e(k)


def local(tokens, routes, slots, gate_weight, up_weight):
    tok_rows, depth = tokens.shape
    units = gate_weight.shape[1]
    hrows = ROWS + COUNT_ROWS
    nk = len(CHUNKS)
    vmem = pl.BlockSpec(memory_space=pltpu.VMEM)
    hbm = pl.BlockSpec(memory_space=pl.ANY)
    dma = pltpu.SemaphoreType.DMA
    cov, means = pl.pallas_call(
        kernel,
        out_shape=(
            jax.ShapeDtypeStruct((units, units), F32),
            jax.ShapeDtypeStruct((1, units), F32),
        ),
        in_specs=[hbm, hbm, hbm, hbm, hbm],
        out_specs=(vmem, vmem),
        scratch_shapes=[
            pltpu.VMEM(tokens.shape, BF16),
            pltpu.VMEM(routes.shape[::-1], jnp.int32),
            pltpu.VMEM(routes.shape[::-1], jnp.int32),
            pltpu.VMEM((XS, CAP, depth + FLAG), BF16),
            pltpu.VMEM((ROWS, depth + FLAG), BF16),
            pltpu.VMEM((depth, units), BF16),
            pltpu.VMEM((depth, units), BF16),
            pltpu.VMEM((ZS, hrows, units), BF16),
            pltpu.VMEM((ZS, hrows, units), BF16),
            pltpu.VMEM((YS - 1, ROWS, units), BF16),
            pltpu.VMEM((units, units + 128), F32),
            pltpu.VMEM((8, 2 * units), F32),
            dma((5,)), dma((nk,)),
            dma((nk,)), dma((nk,)),
            dma((nk, 2, 2)), dma((nk, 2, 2)),
            dma((nk, 2)), dma((nk, 2)),
            dma((nk, 4)), dma((nk, 4)),
            dma((nk, 4, 2)), dma((nk, 4, 2)),
            dma((nk, ZS - 1)), dma((nk, ZS - 1)),
            dma((nk, 2)), dma((nk, 2)), dma((nk, 2)),
            dma((nk, YS - 1)), dma((nk, YS - 1)),
            dma((nk, YS)), dma((nk, ZS)),
            dma((nk,)), dma((nk,)),
        ],
        compiler_params=pltpu.CompilerParams(
            collective_id=0, has_side_effects=True, vmem_limit_bytes=60 << 20
        ),
        name="moments",
    )(tokens, routes.T, slots.T, gate_weight, up_weight)
    return means.reshape(units), cov


def solution(mesh):
    in_specs = (
        P(("dp", "expert"), None),
        P(("dp", "expert"), None),
        P(("dp", "expert"), None),
        P(None, "expert"),
        P(None, "expert"),
    )
    out_specs = (P("expert"), P("expert", "dp"))
    return jax.shard_map(local, mesh=mesh, in_specs=in_specs, out_specs=out_specs, check_vma=False)
```
